32 devices in a mesh: dp: 2 (over y), expert: 16 (over z, x, core).
Axes of the slice: x: 2, y: 2, z: 4, core: 2. Of those that a mesh axis runs over, the one named last changes fastest.
Arguments:
- hidden_in: bfloat16 [4096, 2, 512], P(('dp', 'expert')), may hold values from -6 to 6
- out_grad: bfloat16 [4096, 4096], P(('dp', 'expert')), may hold values from -3 to 3
- expert_ids: int32 [4096, 2], P(('dp', 'expert')), may hold values from 0 to 15, as said below
- gate_num: int32 [4096, 2], P(('dp', 'expert')), may hold values from 1 to 16
- down_weight: bfloat16 [16, 512, 4096], P('expert', 'dp'), may hold values from -0.25 to 0.25
Outputs:
- layer_out: bfloat16 [4096, 4096], P(('dp', 'expert'))
- hidden_grad: bfloat16 [4096, 2, 512], P(('dp', 'expert'))
- down_grad: bfloat16 [16, 512, 4096], P('expert', 'dp')
The draws below stay inside these ranges and needn't reach their ends.
Inputs may be any that keep to these rules, and one draw needn't show every extreme that they name: `expert_ids`: the 2 experts of a token differ. The 128 tokens of one device name any one expert at most 32 times.
All inputs are finite; a program needn't handle non-finite values.
Results may differ from the reference program's by a relative error of at most 0.0059.
Values may be sent and summed in bfloat16 or wider, within the bound.
No kernel may reach another device: no remote copies, remote signals or barrier semaphores. Data moves between devices by JAX's collectives and lax.ppermute only.
A program may use at most 64 MiB of HBM per device.

```python
import jax
import jax.numpy as jnp
from jax import lax

D = 4096
FF = 512
TOP = 2
TOK_DEV = 128
EXPERTS = 16
CAP = 32
REPLICAS = 2
TOKENS = 4096


def draw_expert_ids(key, part):
    blocks = TOKENS // TOK_DEV
    mean_load = 2 * TOK_DEV // EXPERTS
    busiest = jax.random.randint(jax.random.fold_in(key, 11), (), 0, EXPERTS)
    block_keys = jax.random.split(jax.random.fold_in(key, 12), blocks)
    shuffled = jax.vmap(lambda subkey: jax.random.permutation(subkey, EXPERTS))(block_keys).astype(jnp.int32)
    position = jnp.argsort(shuffled, axis=1, stable=True).astype(jnp.int32)
    pair_index = position // 2
    direction = 1 - 2 * (position % 2)
    shift_amount = jax.random.randint(jax.random.fold_in(key, 13), (blocks, EXPERTS // 2), 0, mean_load + 1)
    expert_range = jnp.arange(EXPERTS, dtype=jnp.int32)
    busy_pair = jnp.take(pair_index, busiest, axis=1)
    in_busy = pair_index == busy_pair[:, None]
    direction = jnp.where(in_busy, jnp.where(expert_range[None, :] == busiest, 1, -1), direction)
    amount = jnp.take_along_axis(shift_amount, pair_index, axis=1)
    amount = jnp.where(in_busy, mean_load, amount)
    loads = mean_load + direction * amount
    label_ends = jnp.cumsum(loads, axis=1)
    slot_range = jnp.arange(2 * TOK_DEV, dtype=jnp.int32)
    labels = jnp.sum((label_ends[:, None, :] <= slot_range[None, :, None]).astype(jnp.int32), axis=2)
    first_slot = labels[:, :TOK_DEV]
    second = labels[:, TOK_DEV:]
    swap_bit = jax.random.randint(jax.random.fold_in(key, 14), (blocks, TOK_DEV), 0, 2)
    upper = jnp.where(swap_bit == 1, second, first_slot)
    lower = jnp.where(swap_bit == 1, first_slot, second)
    token_keys = jax.random.split(jax.random.fold_in(key, 15), blocks)
    token_order = jax.vmap(lambda subkey: jax.random.permutation(subkey, TOK_DEV))(token_keys)
    upper = jnp.take_along_axis(upper, token_order, axis=1)
    lower = jnp.take_along_axis(lower, token_order, axis=1)
    return jnp.stack([upper, lower], axis=2).reshape(TOKENS, 2).astype(jnp.int32)


def plant(entries, own_key, low, largest):
    spot = [jax.random.randint(jax.random.fold_in(own_key, axis), (), 0, length) for axis, length in enumerate(entries.shape)]
    longest = entries.shape.index(max(entries.shape))
    next_to = spot[:longest] + [(spot[longest] + 1) % entries.shape[longest]] + spot[longest + 1:]
    return entries.at[tuple(spot)].set(low).at[tuple(next_to)].set(largest)


def steps_of(stream_key, shape, cuts, low, largest):
    loudness, own = 1.0, jax.random.fold_in(stream_key, 6)
    for dim, parts in cuts:
        draws = jnp.exp(jax.random.uniform(jax.random.fold_in(own, dim), (parts,), jnp.float32, low / len(cuts), largest / len(cuts)))
        loudness = loudness * jnp.repeat(draws, shape[dim] // parts).reshape([-1 if axis == dim else 1 for axis in range(len(shape))])
    return loudness


def normal_values(rng, shape, spread, bound, shards=(), kind=jnp.bfloat16):
    factor_of = steps_of(rng, shape, shards, -0.22, 0.18) if shards else 1.0
    drawn = jax.random.normal(rng, shape, jnp.float32) * spread * factor_of
    return jnp.minimum(jnp.maximum(drawn, -bound), bound).astype(kind)


def setup_inputs(seed: int = 0) -> dict:
    seeds = jax.random.split(jax.random.key(seed), 6)
    return {
        "hidden_in": normal_values(seeds[0], (TOKENS, TOP, FF), 1.0, 6.0, ((0, 32),)),
        "out_grad": normal_values(seeds[1], (TOKENS, D), 0.5, 3.0, ((0, 32),)),
        "expert_ids": draw_expert_ids(jax.random.fold_in(seeds[5], 71), 0),
        "gate_num": plant(jax.random.randint(seeds[3], (TOKENS, TOP), 1, 17), jax.random.fold_in(seeds[3], 1), 1, 16).astype(jnp.int32),
        "down_weight": normal_values(seeds[4], (EXPERTS, FF, D), FF ** -0.5, 0.25, ((0, 16), (1, 2))),
    }


def reference(hidden_in, out_grad, expert_ids, gate_num, down_weight):
    numerators = gate_num.astype(jnp.float32)
    gate = numerators / jnp.sum(numerators, axis=1, keepdims=True)
    scaled = (gate[:, :, None] * hidden_in.astype(jnp.float32)).astype(jnp.bfloat16)
    replica_tokens = TOK_DEV * EXPERTS
    slot_total = 2 * replica_tokens
    expert_rows = EXPERTS * CAP

    def replica(grad_sum, replica_index):
        first_token = (replica_index * replica_tokens).astype(jnp.int32)
        scaled_slots = lax.dynamic_slice_in_dim(scaled, first_token, replica_tokens, 0).reshape(slot_total, FF)
        grad_tokens = lax.dynamic_slice_in_dim(out_grad, first_token, replica_tokens, 0)
        routed = lax.dynamic_slice_in_dim(expert_ids, first_token, replica_tokens, 0).reshape(slot_total)
        share_slots = lax.dynamic_slice_in_dim(gate, first_token, replica_tokens, 0).reshape(slot_total)
        sorted_slots = jnp.argsort(routed, stable=True).astype(jnp.int32)
        expert_counts = jnp.sum((routed[:, None] == jnp.arange(EXPERTS, dtype=jnp.int32)[None, :]).astype(jnp.int32), axis=0).astype(jnp.int32)
        expert_starts = (jnp.cumsum(expert_counts) - expert_counts).astype(jnp.int32)
        padded_slots = jnp.concatenate([sorted_slots, jnp.zeros((expert_rows,), jnp.int32)])

        def expert_step(state_pair, expert):
            out_buffer, grad_buffer = state_pair
            begin = expert_starts[expert]
            slot_index = lax.dynamic_slice_in_dim(padded_slots, begin, expert_rows, 0)
            filled = jnp.arange(expert_rows, dtype=jnp.int32) < expert_counts[expert]
            scaled_rows = jnp.where(filled[:, None], scaled_slots[slot_index], jnp.zeros((), jnp.bfloat16))
            grad_rows = jnp.where(filled[:, None], grad_tokens[slot_index // 2], jnp.zeros((), jnp.bfloat16))
            weight = down_weight[expert]
            slot_out = jnp.dot(scaled_rows, weight, preferred_element_type=jnp.float32).astype(jnp.bfloat16)
            back_proj = jnp.dot(grad_rows, weight.T, preferred_element_type=jnp.float32)
            share_rows = jnp.where(filled, share_slots[slot_index], jnp.zeros((), jnp.float32))
            slot_grad = (share_rows[:, None] * back_proj).astype(jnp.bfloat16)
            out_buffer = lax.dynamic_update_slice_in_dim(out_buffer, slot_out, begin, 0)
            grad_buffer = lax.dynamic_update_slice_in_dim(grad_buffer, slot_grad, begin, 0)
            partial_value = jnp.dot(scaled_rows.T, grad_rows, preferred_element_type=jnp.float32).astype(jnp.bfloat16)
            return (out_buffer, grad_buffer), partial_value

        start_pair = (jnp.zeros((slot_total + expert_rows, D), jnp.bfloat16), jnp.zeros((slot_total + expert_rows, FF), jnp.bfloat16))
        (out_buffer, grad_buffer), partials = lax.scan(expert_step, start_pair, jnp.arange(EXPERTS, dtype=jnp.int32))
        inverse = jnp.zeros((slot_total,), jnp.int32).at[sorted_slots].set(jnp.arange(slot_total, dtype=jnp.int32))
        out_slots = out_buffer[inverse].reshape(replica_tokens, 2, D)
        token_out = jnp.sum(out_slots.astype(jnp.float32), axis=1).astype(jnp.bfloat16)
        grad_slots = grad_buffer[inverse].reshape(replica_tokens, 2, FF)
        return grad_sum + partials.astype(jnp.float32), (token_out, grad_slots)

    grad_sum, (outputs, grads) = lax.scan(replica, jnp.zeros((EXPERTS, FF, D), jnp.float32), jnp.arange(REPLICAS, dtype=jnp.int32))
    down_grad = (grad_sum / REPLICAS).astype(jnp.bfloat16)
    return outputs.reshape(TOKENS, D), grads.reshape(TOKENS, TOP, FF), down_grad
```

```python
import jax
import jax.numpy as jnp
from jax import lax
from jax.sharding import Mesh
from jax.sharding import PartitionSpec as P

F32 = jnp.float32
BF16 = jnp.bfloat16
SWAP = [(0, 1), (1, 0)]


def dot(a, b, ca=1, cb=0):
    return lax.dot_general(a, b, (((ca,), (cb,)), ((), ())), preferred_element_type=F32)


def one_hot_rows(rows, index):
    return (jnp.arange(rows, dtype=jnp.int32)[:, None] == index[None, :]).astype(BF16)


def target_rows(expert_ids, experts, capacity):
    routed = expert_ids.reshape(-1)
    slots = routed.shape[0]
    one_hot = (routed[:, None] == jnp.arange(experts, dtype=jnp.int32)[None, :]).astype(BF16)
    order = jnp.arange(slots, dtype=jnp.int32)
    earlier = (order[:, None] > order[None, :]).astype(BF16)
    ordinal = jnp.sum(dot(earlier, one_hot) * one_hot.astype(F32), axis=1).astype(jnp.int32)
    return (routed * capacity + ordinal).reshape(expert_ids.shape)


def exchange(x, axes):
    return lax.all_to_all(x, axes, split_axis=0, concat_axis=0, tiled=True)


def swap_if(flag, x):
    n = x.shape[0] // 2
    low, high = x[:n], x[n:]
    return jnp.where(flag, jnp.concatenate([high, low], 0), x)


def on_device(hidden_in, out_grad, expert_ids, gate_num, down_weight):
    tok_rows, top, units = hidden_in.shape
    half_experts = lax.axis_size("e")
    experts = 2 * half_experts
    replicas = lax.axis_size("dp")
    capacity = 4 * tok_rows // experts
    half_rows = half_experts * capacity
    slots = top * tok_rows
    side = lax.axis_index("h")
    dp = lax.axis_index("dp")
    share_units = units // replicas

    ids_other = lax.ppermute(expert_ids, "h", SWAP)
    grad_other = lax.ppermute(out_grad, "h", SWAP)
    weight_own = down_weight[0]
    if replicas == 2:
        weights = [weight_own, lax.ppermute(weight_own, "dp", SWAP)]
    else:
        weights = [lax.all_gather(weight_own, "dp", axis=0, tiled=True)]

    rows_own = target_rows(expert_ids, experts, capacity)
    rows_other = target_rows(ids_other, experts, capacity)
    numerators = gate_num.astype(F32)
    gate = numerators / jnp.sum(numerators, axis=1, keepdims=True)
    scaled = (gate[:, :, None] * hidden_in.astype(F32)).astype(BF16).reshape(slots, units)
    if replicas == 2:
        scaled = jnp.where(
            dp == 1,
            jnp.concatenate([scaled[:, share_units:], scaled[:, :share_units]], 1),
            scaled,
        )
    send_hidden = dot(one_hot_rows(2 * half_rows, rows_own.reshape(slots)), scaled).astype(BF16)
    recv_hidden = exchange(send_hidden, ("h", "e"))
    recv_hidden = swap_if(side == 1, recv_hidden)
    hid = [recv_hidden[:half_rows], recv_hidden[half_rows:]]

    def pick(rows):
        local = rows - side * half_rows
        return one_hot_rows(half_rows, local[:, 0]) + one_hot_rows(half_rows, local[:, 1])

    pick_own = pick(rows_own)
    pick_other = pick(rows_other)
    recv_own = exchange(dot(pick_own, out_grad).astype(BF16), "e")
    recv_other = exchange(dot(pick_other, grad_other).astype(BF16), "e")

    def forward(h):
        if replicas == 2:
            a = dot(h[:, :share_units], weights[0]) + dot(h[:, share_units:], weights[1])
        else:
            a = dot(h, weights[0])
        return a.astype(BF16)

    back_other = exchange(forward(hid[1]), "e")
    part_other = dot(pick_other, back_other, 0, 0).astype(BF16)
    part_mine = lax.ppermute(part_other, "h", SWAP)
    back_own = exchange(forward(hid[0]), "e")
    layer_out = (dot(pick_own, back_own, 0, 0) + part_mine.astype(F32)).astype(BF16)

    def backward(g):
        return jnp.concatenate([dot(g, w, 1, 1).astype(BF16) for w in weights], 1)

    grad_rows = swap_if(
        side == 1, jnp.concatenate([backward(recv_own), backward(recv_other)], 0)
    )
    back_rows = exchange(grad_rows, ("h", "e"))
    slot_back = dot(one_hot_rows(2 * half_rows, rows_own.reshape(slots)), back_rows, 0, 0)
    if replicas == 2:
        slot_back = jnp.where(
            dp == 1,
            jnp.concatenate([slot_back[:, share_units:], slot_back[:, :share_units]], 1),
            slot_back,
        )
    hidden_grad = (gate[:, :, None] * slot_back.reshape(tok_rows, top, units)).astype(BF16)

    def weight_grad(lo, hi):
        return (
            dot(hid[0][:, lo:hi], recv_own, 0, 0) + dot(hid[1][:, lo:hi], recv_other, 0, 0)
        ).astype(BF16)

    if replicas == 2:
        theirs = lax.ppermute(weight_grad(share_units, units), "dp", SWAP)
        total = weight_grad(0, share_units).astype(F32) + theirs.astype(F32)
    else:
        total = lax.psum_scatter(
            weight_grad(0, units), "dp", scatter_dimension=0, tiled=True
        ).astype(F32)
    down_grad = (total / replicas).astype(BF16)[None]
    return (layer_out, hidden_grad, down_grad)


def solution(mesh):
    replicas, experts = mesh.devices.shape
    halves = Mesh(mesh.devices.reshape(replicas, 2, experts // 2), ("dp", "h", "e"))
    tokens = ("dp", "h", "e")
    return jax.shard_map(
        on_device,
        mesh=halves,
        in_specs=(
            P(tokens, None, None),
            P(tokens, None),
            P(tokens, None),
            P(tokens, None),
            P(("h", "e"), "dp", None),
        ),
        out_specs=(
            P(tokens, None),
            P(tokens, None, None),
            P(("h", "e"), "dp", None),
        ),
        check_vma=False,
    )
```

```python
import functools

import jax
import jax.numpy as jnp
from jax import lax
from jax.experimental import pallas as pl
from jax.experimental.pallas import tpu as pltpu
from jax.sharding import Mesh
from jax.sharding import PartitionSpec as P

F32 = jnp.float32
BF16 = jnp.bfloat16
I32 = jnp.int32
SWAP = [(0, 1), (1, 0)]
VMEM = pl.BlockSpec(memory_space=pltpu.VMEM)
SMEM = pl.BlockSpec(memory_space=pltpu.SMEM)
STEP = 1024


def dot(a, b, ca=1, cb=0):
    return lax.dot_general(a, b, (((ca,), (cb,)), ((), ())), preferred_element_type=F32)


def call(body, outs, *args, specs=None):
    many = isinstance(outs, (list, tuple))
    return pl.pallas_call(
        body,
        out_shape=outs,
        in_specs=[SMEM] + [VMEM] * (len(args) - 1),
        out_specs=[VMEM] * len(outs) if many else VMEM,
        compiler_params=pltpu.CompilerParams(vmem_limit_bytes=48 * 1024 * 1024),
    )(*args)


def shaped(shape, dtype=BF16):
    return jax.ShapeDtypeStruct(tuple(shape), dtype)


def iota(shape, dim):
    return lax.broadcasted_iota(I32, shape, dim)


def slot_rows(ids, experts, capacity):
    tokens = ids.shape[0]
    lanes = iota((tokens, experts), 1)
    earlier = (iota((tokens, tokens), 0) > iota((tokens, tokens), 1)).astype(BF16)
    eye = iota((tokens, tokens), 0) == iota((tokens, tokens), 1)
    cols, rows = [], []
    base = jnp.zeros((1, experts), F32)
    for k in range(ids.shape[1]):
        chosen = ids[:, k : k + 1]
        one_hot = (chosen == lanes).astype(F32)
        before = dot(earlier, one_hot.astype(BF16)) + base
        ordinal = jnp.sum(before * one_hot, axis=1, keepdims=True)
        base = base + jnp.sum(one_hot, axis=0, keepdims=True)
        col = chosen.astype(F32) * capacity + ordinal
        row = jnp.sum(jnp.where(eye, jnp.broadcast_to(col, (tokens, tokens)), 0.0), axis=0, keepdims=True)
        cols.append(col.astype(I32))
        rows.append(row.astype(I32))
    return cols, rows


def store_rows(cols, rows, row_ref, col_ref):
    for k in range(len(cols)):
        row_ref[k : k + 1, :] = rows[k]
        col_ref[:, k : k + 1] = cols[k]


def swap_halves(x, flag):
    n = x.shape[1] // 2
    return jnp.where(flag, jnp.concatenate([x[:, n:], x[:, :n]], 1), x)


def prepare_body(experts, capacity, top, swap, place, ids_ref, num_ref, hid_ref, row_ref, col_ref, send_ref):
    tokens = ids_ref.shape[0]
    units = hid_ref.shape[1] // top
    cols, rows = slot_rows(ids_ref[...], experts, capacity)
    store_rows(cols, rows, row_ref, col_ref)
    numerators = num_ref[...].astype(F32)
    total = jnp.sum(numerators, axis=1, keepdims=True)
    target = iota((experts * capacity, tokens), 0)
    acc = None
    for k in range(top):
        share = numerators[:, k : k + 1] / total
        scaled = (share * hid_ref[:, k * units : (k + 1) * units].astype(F32)).astype(BF16)
        part = dot((target == rows[k]).astype(BF16), scaled)
        acc = part if acc is None else acc + part
    out = acc.astype(BF16)
    send_ref[...] = swap_halves(out, place[1] == 1) if swap else out


def rows_body(experts, capacity, place, ids_ref, row_ref, col_ref):
    cols, rows = slot_rows(ids_ref[...], experts, capacity)
    store_rows(cols, rows, row_ref, col_ref)


def pick_body(top, place, row_ref, *refs):
    *grads, out_ref = refs
    half = out_ref.shape[0]
    target = iota((half, row_ref.shape[1]), 0) + place[0] * half
    pick = None
    for k in range(top):
        hit = target == row_ref[k : k + 1, :]
        pick = hit if pick is None else pick | hit
    pick = pick.astype(BF16)
    c0 = 0
    for g in grads:
        width = g.shape[1]
        step = min(STEP, width)
        for c in range(0, width, step):
            out_ref[:, c0 + c : c0 + c + step] = dot(pick, g[:, c : c + step]).astype(BF16)
        c0 += width


def combine_body(top, place, col_ref, back_ref, *refs):
    *parts, out_refs = refs
    half, width = back_ref.shape
    target = iota((col_ref.shape[0], half), 1) + place[0] * half
    hit = None
    for k in range(top):
        h = target == col_ref[:, k : k + 1]
        hit = h if hit is None else hit | h
    hit = hit.astype(BF16)
    step = min(STEP, width)
    for c in range(0, width, step):
        acc = dot(hit, back_ref[:, c : c + step])
        c0 = 0
        for p in parts:
            if c0 <= c < c0 + p.shape[1]:
                acc = acc + p[:, c - c0 : c - c0 + step].astype(F32)
            c0 += p.shape[1]
        out_refs[:, c : c + step] = acc.astype(BF16)


def piece_cols(pieces, c, step):
    for r0, c0, ref in pieces:
        if c0 <= c < c0 + ref.shape[1]:
            yield r0, ref.shape[0], ref[:, c - c0 : c - c0 + step]


def forward_body(which, offsets, place, hid_ref, *refs):
    *weights, out_ref = refs
    half, width = out_ref.shape
    side = place[0]
    start = (1 - side if which else side) * half
    hid = hid_ref[pl.ds(pl.multiple_of(start, half), half), :]
    pieces = [(r, c, ref) for (r, c), ref in zip(offsets, weights)]
    step = min(STEP, width)
    for c in range(0, width, step):
        acc = None
        for r0, n, w in piece_cols(pieces, c, step):
            part = dot(hid[:, r0 : r0 + n], w)
            acc = part if acc is None else acc + part
        out_ref[:, c : c + step] = acc.astype(BF16)


def backward_body(offsets, place, own_ref, other_ref, *refs):
    *weights, out_ref = refs
    half, width = own_ref.shape
    side = place[0]
    pieces = [(r, c, ref) for (r, c), ref in zip(offsets, weights)]
    starts = sorted({r for r, _ in offsets})
    for which, g in ((0, own_ref), (1, other_ref)):
        start = pl.multiple_of((1 - side if which else side) * half, half)
        for r in starts:
            acc, n = None, 0
            for r0, c0, ref in pieces:
                if r0 == r:
                    part = dot(g[:, c0 : c0 + ref.shape[1]], ref[...], 1, 1)
                    acc = part if acc is None else acc + part
                    n = ref.shape[0]
            out_ref[pl.ds(start, half), r : r + n] = acc.astype(BF16)


def weight_grad_body(lo, hi, place, hid_ref, own_ref, other_ref, *out_refs):
    half, _ = own_ref.shape
    side = place[0]
    h_own = hid_ref[pl.ds(pl.multiple_of(side * half, half), half), :][:, lo:hi]
    h_other = hid_ref[pl.ds(pl.multiple_of((1 - side) * half, half), half), :][:, lo:hi]
    c0 = 0
    for out_ref in out_refs:
        width = out_ref.shape[1]
        step = min(STEP, width)
        for c in range(0, width, step):
            at = slice(c0 + c, c0 + c + step)
            acc = dot(h_own, own_ref[:, at], 0, 0) + dot(h_other, other_ref[:, at], 0, 0)
            out_ref[:, c : c + step] = acc.astype(BF16)
        c0 += width


def average_body(lo, hi, replicas, place, hid_ref, own_ref, other_ref, *refs):
    *theirs, out_ref = refs
    half, _ = own_ref.shape
    side = place[0]
    h_own = hid_ref[pl.ds(pl.multiple_of(side * half, half), half), :][:, lo:hi]
    h_other = hid_ref[pl.ds(pl.multiple_of((1 - side) * half, half), half), :][:, lo:hi]
    c0 = 0
    for t in theirs:
        width = t.shape[1]
        step = min(STEP, width)
        for c in range(0, width, step):
            at = slice(c0 + c, c0 + c + step)
            acc = dot(h_own, own_ref[:, at], 0, 0) + dot(h_other, other_ref[:, at], 0, 0)
            acc = acc.astype(BF16).astype(F32) + t[:, c : c + step].astype(F32)
            out_ref[:, at] = (acc / replicas).astype(BF16)
        c0 += width


def hidden_grad_body(top, swap, place, col_ref, num_ref, back_ref, out_ref):
    tokens = col_ref.shape[0]
    rows, units = back_ref.shape
    numerators = num_ref[...].astype(F32)
    total = jnp.sum(numerators, axis=1, keepdims=True)
    target = iota((tokens, rows), 1)
    for k in range(top):
        hit = (target == col_ref[:, k : k + 1]).astype(BF16)
        got = (numerators[:, k : k + 1] / total * dot(hit, back_ref[...])).astype(BF16)
        out_ref[:, k * units : (k + 1) * units] = swap_halves(got, place[1] == 1) if swap else got


def after(x, *others):
    return lax.optimization_barrier((x, *others))[0]


def exchange(x, axes):
    return lax.all_to_all(x, axes, split_axis=0, concat_axis=0, tiled=True)


def cut(x, *shares):
    total, at, out = sum(shares), 0, []
    for s in shares:
        n = x.shape[1] * s // total
        out.append(x[:, at : at + n])
        at += n
    return out


def on_device(hidden_in, out_grad, expert_ids, gate_num, down_weight):
    tokens, top, units = hidden_in.shape
    width = out_grad.shape[1]
    half_experts = lax.axis_size("e")
    experts = 2 * half_experts
    replicas = lax.axis_size("dp")
    capacity = 4 * tokens // experts
    half = half_experts * capacity
    share = units // replicas
    pair = replicas == 2
    place = jnp.stack([lax.axis_index("h"), lax.axis_index("dp")]).astype(I32)
    part = functools.partial
    row_shape, col_shape = shaped((top, tokens), I32), shaped((tokens, top), I32)

    def to_other(x):
        return lax.ppermute(x, "h", SWAP)

    def to_replica(x):
        return lax.ppermute(x, "dp", SWAP)

    weight = down_weight[0]
    ids_other = to_other(expert_ids)
    row_own, col_own, send_hidden = call(
        part(prepare_body, experts, capacity, top, pair),
        [row_shape, col_shape, shaped((2 * half, units))],
        place, expert_ids, gate_num, hidden_in.reshape(tokens, top * units),
    )
    row_other, col_other = call(
        part(rows_body, experts, capacity), [row_shape, col_shape], place, ids_other
    )
    send_own = call(part(pick_body, top), shaped((half, width)), place, row_own, out_grad)

    if pair:
        w_a, w_b, w_c = cut(weight, 1, 1, 2)
        w_a = to_replica(w_a)
        hid = exchange(after(send_hidden, w_a), ("h", "e"))
        w_b = to_replica(w_b)
    else:
        hid = exchange(send_hidden, ("h", "e"))
    g_a, g_b, g_c = cut(out_grad, 1, 2, 1)
    g_a = to_other(g_a)
    if pair:
        recv_own = exchange(after(send_own, hid, w_b, g_a), "e")
        w_c = to_replica(w_c)
        q = width // 4
        weights = [weight, w_a, w_b, w_c]
        offsets = [(0, 0), (share, 0), (share, q), (share, 2 * q)]
    else:
        recv_own = exchange(after(send_own, hid, g_a), "e")
        weights = [lax.all_gather(weight, "dp", axis=0, tiled=True)]
        offsets = [(0, 0)]
    g_b = to_other(g_b)
    out_other = call(part(forward_body, 1, offsets), shaped((half, width)), place, hid, *weights)
    back_other = exchange(after(out_other, recv_own, g_b), "e")
    g_c = to_other(g_c)
    send_other = call(part(pick_body, top), shaped((half, width)), place, row_other, g_a, g_b, g_c)
    recv_other = exchange(after(send_other, back_other), "e")
    part_other = call(part(combine_body, top), shaped((tokens, width)), place, col_other, back_other)
    p_a, p_b = cut(part_other, 1, 1)
    p_a = to_other(p_a)
    out_own = call(part(forward_body, 0, offsets), shaped((half, width)), place, hid, *weights)
    back_own = exchange(after(out_own, recv_other, p_a), "e")
    p_b = to_other(p_b)
    if pair:
        d_a, d_b = call(
            part(weight_grad_body, share, units),
            [shaped((share, width // 2))] * 2,
            place, hid, recv_own, recv_other,
        )
        d_a = to_replica(d_a)
    grad_rows = call(
        part(backward_body, offsets), shaped((2 * half, units)),
        place, recv_own, recv_other, *weights,
    )
    gate_on = (back_own, p_b, d_a) if pair else (back_own, p_b)
    back_rows = exchange(after(grad_rows, *gate_on), ("h", "e"))
    layer_out = call(
        part(combine_body, top), shaped((tokens, width)), place, col_own, back_own, p_a, p_b
    )
    if pair:
        d_b = to_replica(d_b)
        down_grad = call(
            part(average_body, 0, share, replicas), shaped((share, width)),
            place, hid, recv_own, recv_other, d_a, d_b,
        )
    else:
        whole = call(
            part(weight_grad_body, 0, units), [shaped((units, width))],
            place, hid, recv_own, recv_other,
        )[0]
        total = lax.psum_scatter(whole, "dp", scatter_dimension=0, tiled=True)
        down_grad = (total.astype(F32) / replicas).astype(BF16)
    hidden_grad = call(
        part(hidden_grad_body, top, pair), shaped((tokens, top * units)),
        place, col_own, gate_num, back_rows,
    )
    return (layer_out, hidden_grad.reshape(tokens, top, units), down_grad[None])


def solution(mesh):
    replicas, experts = mesh.devices.shape
    halves = Mesh(mesh.devices.reshape(replicas, 2, experts // 2), ("dp", "h", "e"))
    tokens = ("dp", "h", "e")
    return jax.shard_map(
        on_device,
        mesh=halves,
        in_specs=(
            P(tokens, None, None),
            P(tokens, None),
            P(tokens, None),
            P(tokens, None),
            P(("h", "e"), "dp", None),
        ),
        out_specs=(
            P(tokens, None),
            P(tokens, None, None),
            P(("h", "e"), "dp", None),
        ),
        check_vma=False,
    )
```

```python
import functools

import jax
import jax.numpy as jnp
from jax import lax
from jax.experimental import pallas as pl
from jax.experimental.pallas import tpu as pltpu
from jax.sharding import Mesh
from jax.sharding import PartitionSpec as P

F32 = jnp.float32
BF16 = jnp.bfloat16
I32 = jnp.int32
VMEM = pl.BlockSpec(memory_space=pltpu.VMEM)
SMEM = pl.BlockSpec(memory_space=pltpu.SMEM)
STEP = 1024
PLANES = 4
PAIR = 2
COST = 1 << 38


def dot(a, b, ca=1, cb=0):
    return lax.dot_general(a, b, (((ca,), (cb,)), ((), ())), preferred_element_type=F32)


def call(body, outs, *args, cost=0, scratch=()):
    many = isinstance(outs, (list, tuple))
    return pl.pallas_call(
        body,
        out_shape=outs,
        in_specs=[SMEM] + [VMEM] * (len(args) - 1),
        out_specs=[VMEM] * len(outs) if many else VMEM,
        scratch_shapes=scratch,
        name=(body.func if isinstance(body, functools.partial) else body).__name__,
        cost_estimate=pl.CostEstimate(flops=cost, bytes_accessed=0, transcendentals=0),
        compiler_params=pltpu.CompilerParams(vmem_limit_bytes=16 * 1024 * 1024),
    )(*args)


def shaped(shape, dtype=BF16):
    return jax.ShapeDtypeStruct(tuple(shape), dtype)


def iota(shape, dim):
    return lax.broadcasted_iota(I32, shape, dim)


def steps(width):
    step = min(STEP, width)
    return [slice(c, c + step) for c in range(0, width, step)]


def slot_rows(ids, experts, capacity):
    tokens = ids.shape[0]
    lanes = iota((tokens, experts), 1)
    earlier = (iota((tokens, tokens), 0) > iota((tokens, tokens), 1)).astype(BF16)
    eye = iota((tokens, tokens), 0) == iota((tokens, tokens), 1)
    cols, rows = [], []
    base = jnp.zeros((1, experts), F32)
    for k in range(ids.shape[1]):
        chosen = ids[:, k : k + 1]
        one_hot = (chosen == lanes).astype(F32)
        before = dot(earlier, one_hot.astype(BF16)) + base
        ordinal = jnp.sum(before * one_hot, axis=1, keepdims=True)
        base = base + jnp.sum(one_hot, axis=0, keepdims=True)
        col = chosen.astype(F32) * capacity + ordinal
        row = jnp.sum(jnp.where(eye, jnp.broadcast_to(col, (tokens, tokens)), 0.0), axis=0, keepdims=True)
        cols.append(col.astype(I32))
        rows.append(row.astype(I32))
    return cols, rows


def swap_halves(x, flag):
    n = x.shape[1] // 2
    return jnp.where(flag, jnp.concatenate([x[:, n:], x[:, :n]], 1), x)


def prepare_body(experts, capacity, top, swap, place, ids_ref, num_ref, hid_ref, row_ref, col_ref, send_ref):
    tokens = ids_ref.shape[0]
    units = hid_ref.shape[1] // top
    cols, rows = slot_rows(ids_ref[...], experts, capacity)
    numerators = num_ref[...].astype(F32)
    total = jnp.sum(numerators, axis=1, keepdims=True)
    target = iota((experts * capacity, tokens), 0)
    acc = None
    for k in range(top):
        row_ref[k : k + 1, :] = rows[k]
        col_ref[:, k : k + 1] = cols[k]
        share = numerators[:, k : k + 1] / total
        scaled = (share * hid_ref[:, k * units : (k + 1) * units].astype(F32)).astype(BF16)
        part = dot((target == rows[k]).astype(BF16), scaled)
        acc = part if acc is None else acc + part
    out = acc.astype(BF16)
    send_ref[...] = swap_halves(out, place[1] == 1) if swap else out


def rows_body(experts, capacity, place, *refs):
    ids_refs, row_refs = refs[:PLANES], refs[PLANES:]
    found = [slot_rows(ref[...], experts, capacity)[1] for ref in ids_refs]
    for i, row_ref in enumerate(row_refs):
        for k in range(row_ref.shape[0]):
            row = found[PLANES - 1][k]
            for j in range(PLANES - 1):
                row = jnp.where((place[0] ^ i) == j, found[j][k], row)
            row_ref[k : k + 1, :] = row


def picks(place, peers, capacity, row_refs):
    r = iota((peers * PAIR * capacity, 1), 0)
    peer = r // (PAIR * capacity)
    which = (r // capacity) % PAIR
    target = (place[0] * peers + peer) * capacity + r % capacity
    blocks = []
    for j, row_ref in enumerate(row_refs):
        hit = None
        for k in range(row_ref.shape[0]):
            h = target == row_ref[k : k + 1, :]
            hit = h if hit is None else hit | h
        blocks.append((hit & (which == j)).astype(BF16))
    return jnp.concatenate(blocks, 1)


def pick_body(peers, capacity, offset, place, *refs):
    *row_refs, grad_ref, out_ref = refs
    tokens = row_refs[0].shape[1]
    n = PAIR * capacity
    groups = PLANES // PAIR
    for g in range(groups):
        pick = picks(place, peers, capacity, row_refs[g * PAIR : (g + 1) * PAIR])
        for at in steps(out_ref.shape[1]):
            cols = slice(offset + at.start, offset + at.stop)
            res = dot(pick, grad_ref[g * PAIR * tokens : (g + 1) * PAIR * tokens, cols]).astype(BF16)
            for k in range(peers):
                o = (k * groups + g) * n
                out_ref[o : o + n, at] = res[k * n : (k + 1) * n]


def combine_body(peers, capacity, place, *refs):
    *row_refs, back_ref, out_ref = refs
    tokens = row_refs[0].shape[1]
    n = PAIR * capacity
    groups = PLANES // PAIR
    for g in range(groups):
        pick = picks(place, peers, capacity, row_refs[g * PAIR : (g + 1) * PAIR])
        for at in steps(out_ref.shape[1]):
            rows = [back_ref[(k * groups + g) * n : (k * groups + g + 1) * n, at] for k in range(peers)]
            both = dot(pick, jnp.concatenate(rows, 0), 0, 0).astype(BF16)
            out_ref[g * PAIR * tokens : (g + 1) * PAIR * tokens, at] = both


def reorder(x, outer, inner, capacity):
    return jnp.concatenate(
        [
            x[(a * inner + b) * capacity : (a * inner + b + 1) * capacity]
            for b in range(inner)
            for a in range(outer)
        ],
        0,
    )


def arrange_body(peers, capacity, place, hid_ref, out_ref):
    out_ref[...] = reorder(hid_ref[...].astype(F32), PLANES, peers, capacity).astype(BF16)


def forward_body(offset, place, hid_ref, *refs):
    *weights, out_ref = refs
    hid = hid_ref[...]
    for at in steps(out_ref.shape[1]):
        acc, r = None, 0
        for i, w in enumerate(weights):
            o = offset if i == 0 else 0
            part = dot(hid[:, r : r + w.shape[0]], w[:, o + at.start : o + at.stop])
            acc = part if acc is None else acc + part
            r += w.shape[0]
        out_ref[:, at] = acc.astype(BF16)


def weight_grad_body(lo, hi, place, hid_ref, grad_ref, out_ref):
    for at in steps(out_ref.shape[1]):
        out_ref[:, at] = dot(hid_ref[:, lo:hi], grad_ref[:, at], 0, 0).astype(BF16)


def average_body(replicas, place, *refs):
    *pieces, out_ref = refs
    n = len(pieces) // 2
    c = 0
    for a, b in zip(pieces[:n], pieces[n:]):
        for at in steps(a.shape[1]):
            total = a[:, at].astype(F32) + b[:, at].astype(F32)
            out_ref[:, c + at.start : c + at.stop] = (total / replicas).astype(BF16)
        c += a.shape[1]


def back_dots(grad_ref, weights, offset):
    w = weights[0][:, offset : offset + grad_ref.shape[1]]
    return [dot(grad_ref[...], w, 1, 1)] + [dot(grad_ref[...], x[...], 1, 1) for x in weights[1:]]


def backward_first_body(offset, place, grad_ref, *refs):
    *weights, out_ref = refs
    r = 0
    for part in back_dots(grad_ref, weights, offset):
        out_ref[:, r : r + part.shape[1]] = part
        r += part.shape[1]


def backward_last_body(peers, capacity, offset, place, first_ref, grad_ref, *refs):
    *weights, out_ref = refs
    r = 0
    for part in back_dots(grad_ref, weights, offset):
        m = part.shape[1]
        total = first_ref[:, r : r + m] + part
        out_ref[:, r : r + m] = reorder(total, peers, PLANES, capacity).astype(BF16)
        r += m


def hidden_grad_body(top, swap, place, col_ref, num_ref, back_ref, out_ref):
    tokens = col_ref.shape[0]
    rows, units = back_ref.shape
    numerators = num_ref[...].astype(F32)
    total = jnp.sum(numerators, axis=1, keepdims=True)
    target = iota((tokens, rows), 1)
    for k in range(top):
        hit = (target == col_ref[:, k : k + 1]).astype(BF16)
        got = (numerators[:, k : k + 1] / total * dot(hit, back_ref[...])).astype(BF16)
        out_ref[:, k * units : (k + 1) * units] = swap_halves(got, place[1] == 1) if swap else got


def after(x, *others):
    return lax.optimization_barrier((x, *others))[0]


def exchange(x, axes):
    return lax.all_to_all(x, axes, split_axis=0, concat_axis=0, tiled=True)


def cut(x, n):
    m = x.shape[1] // n
    return [x[:, i * m : (i + 1) * m] for i in range(n)]


def on_device(hidden_in, out_grad, expert_ids, gate_num, down_weight):
    tokens, top, units = hidden_in.shape
    width = out_grad.shape[1]
    peers = lax.axis_size("p")
    experts = PLANES * peers
    replicas = lax.axis_size("dp")
    capacity = 4 * tokens // experts
    share = units // replicas
    pair = replicas == 2
    z = lax.axis_index("z")
    place = jnp.stack([lax.axis_index("z"), lax.axis_index("dp"), lax.axis_index("p")]).astype(I32)
    part = functools.partial
    row_shape, col_shape = shaped((top, tokens), I32), shaped((tokens, top), I32)
    piece = width // 2
    total_rows = experts * capacity

    def to_replica(x):
        return lax.ppermute(x, "dp", [(0, 1), (1, 0)])

    weight = down_weight[0]
    if pair:
        w_a = cut(weight, 2)[0]
        mine = weight
    else:
        theirs = []
        mine = lax.all_gather(weight, "dp", axis=0, tiled=True)

    row_own, col_own, send_hidden = call(
        part(prepare_body, experts, capacity, top, pair),
        [row_shape, col_shape, shaped((total_rows, units))],
        place, expert_ids, gate_num, hidden_in.reshape(tokens, top * units),
    )
    grads = lax.all_gather(out_grad, "z", axis=0, tiled=True)
    if pair:
        theirs = [to_replica(w_a), to_replica(cut(after(weight, send_hidden), 2)[1])]
    hid = exchange(send_hidden, ("z", "p"))
    hid = call(part(arrange_body, peers, capacity), shaped((total_rows, units)), place, hid)
    near = [expert_ids] + [
        lax.ppermute(expert_ids, "z", [(i, i ^ j) for i in range(PLANES)]) for j in range(1, PLANES)
    ]
    chunk = shaped((total_rows, piece))

    def forward(c):
        weights = [mine] + ([theirs[c]] if pair else [])
        return call(part(forward_body, c * piece), chunk, place, hid, *weights, cost=COST)

    def combine(rows, x):
        return call(
            part(combine_body, peers, capacity), shaped((PLANES * tokens, piece)), place, *rows, x
        )

    def reduce(x):
        return lax.psum_scatter(x, "z", scatter_dimension=0, tiled=True)

    def pick(rows, c):
        return call(part(pick_body, peers, capacity, c * piece), chunk, place, *rows, grads, cost=COST)

    def weight_grad(x, lo, hi, cost=0):
        return call(
            part(weight_grad_body, lo, hi), shaped((hi - lo, piece)), place, hid, x, cost=cost
        )

    out_a, out_b = forward(0), forward(1)
    done_a = after(exchange(out_a, "p"), out_b)
    done_b = exchange(after(out_b, done_a), "p")
    rows = call(
        part(rows_body, experts, capacity), [row_shape] * PLANES, after(place, done_a), *near
    )
    part_a = combine(rows, done_a)
    pick_a = pick(rows, 0)
    done_b = after(done_b, part_a)
    layer_a = reduce(after(part_a, done_b))
    sent_a = exchange(after(pick_a, done_b), "p")
    part_b = combine(rows, done_b)
    layer_b = reduce(part_b)
    pick_b = pick(rows, 1)
    sent_a = after(sent_a, part_b, pick_b)
    sent_b = exchange(after(pick_b, sent_a), "p")
    lo, hi = (share, units) if pair else (0, units)
    other_a = weight_grad(sent_a, lo, hi)
    own_a = weight_grad(sent_a, 0, share) if pair else jnp.zeros((share, piece), BF16)
    first = call(
        part(backward_first_body, 0), shaped((total_rows, units), F32), place, sent_a, mine, *theirs[:1]
    )
    sent_b = after(sent_b, other_a, own_a, first)
    other_b = weight_grad(sent_b, lo, hi)
    grad_rows = call(
        part(backward_last_body, peers, capacity, piece), shaped((total_rows, units)),
        after(place, other_b), first, sent_b, mine, *theirs[1:],
    )
    back_rows = exchange(grad_rows, ("z", "p"))
    if pair:
        own_b = weight_grad(after(sent_b, grad_rows), 0, share, cost=COST)
    else:
        own_b = jnp.zeros((share, piece), BF16)
    other_grads, own_grads, back = [other_a, other_b], [own_a, own_b], [layer_a, layer_b]
    if pair:
        other_grads = [to_replica(g) for g in other_grads]
    else:
        other_grads = [
            lax.psum_scatter(g, "dp", scatter_dimension=0, tiled=True) for g in other_grads
        ]

    layer_out = jnp.concatenate([after(x, own_b) for x in back], 1)
    down_grad = call(
        part(average_body, replicas), shaped((share, width)), after(place, layer_out), *own_grads, *other_grads
    )
    hidden_grad = call(
        part(hidden_grad_body, top, pair), shaped((tokens, top * units)), after(place, down_grad), col_own, gate_num, back_rows
    )
    return (layer_out, hidden_grad.reshape(tokens, top, units), down_grad[None])


def solution(mesh):
    replicas, experts = mesh.devices.shape
    planes = Mesh(mesh.devices.reshape(replicas, PLANES, experts // PLANES), ("dp", "z", "p"))
    tokens = ("dp", "z", "p")
    return jax.shard_map(
        on_device,
        mesh=planes,
        in_specs=(
            P(tokens, None, None),
            P(tokens, None),
            P(tokens, None),
            P(tokens, None),
            P(("z", "p"), "dp", None),
        ),
        out_specs=(
            P(tokens, None),
            P(tokens, None, None),
            P(("z", "p"), "dp", None),
        ),
        check_vma=False,
    )
```

```python
import functools

import jax
import jax.numpy as jnp
from jax import lax
from jax.experimental import pallas as pl
from jax.experimental.pallas import tpu as pltpu
from jax.sharding import Mesh
from jax.sharding import PartitionSpec as P

F32 = jnp.float32
BF16 = jnp.bfloat16
I32 = jnp.int32
VMEM = pl.BlockSpec(memory_space=pltpu.VMEM)
SMEM = pl.BlockSpec(memory_space=pltpu.SMEM)
STEP = 1024
PLANES = 4
PAIR = 2
COST = 1 << 38


def dot(a, b, ca=1, cb=0):
    return lax.dot_general(a, b, (((ca,), (cb,)), ((), ())), preferred_element_type=F32)


def call(body, outs, *args, cost=0, scratch=()):
    many = isinstance(outs, (list, tuple))
    return pl.pallas_call(
        body,
        out_shape=outs,
        in_specs=[SMEM] + [VMEM] * (len(args) - 1),
        out_specs=[VMEM] * len(outs) if many else VMEM,
        scratch_shapes=scratch,
        name=(body.func if isinstance(body, functools.partial) else body).__name__,
        cost_estimate=pl.CostEstimate(flops=cost, bytes_accessed=0, transcendentals=0),
        compiler_params=pltpu.CompilerParams(vmem_limit_bytes=16 * 1024 * 1024),
    )(*args)


def shaped(shape, dtype=BF16):
    return jax.ShapeDtypeStruct(tuple(shape), dtype)


def iota(shape, dim):
    return lax.broadcasted_iota(I32, shape, dim)


def steps(width):
    step = min(STEP, width)
    return [slice(c, c + step) for c in range(0, width, step)]


def slot_rows(ids, experts, capacity):
    tokens = ids.shape[0]
    lanes = iota((tokens, experts), 1)
    earlier = (iota((tokens, tokens), 0) > iota((tokens, tokens), 1)).astype(BF16)
    eye = iota((tokens, tokens), 0) == iota((tokens, tokens), 1)
    cols, rows = [], []
    base = jnp.zeros((1, experts), F32)
    for k in range(ids.shape[1]):
        chosen = ids[:, k : k + 1]
        one_hot = (chosen == lanes).astype(F32)
        before = dot(earlier, one_hot.astype(BF16)) + base
        ordinal = jnp.sum(before * one_hot, axis=1, keepdims=True)
        base = base + jnp.sum(one_hot, axis=0, keepdims=True)
        col = chosen.astype(F32) * capacity + ordinal
        row = jnp.sum(jnp.where(eye, jnp.broadcast_to(col, (tokens, tokens)), 0.0), axis=0, keepdims=True)
        cols.append(col.astype(I32))
        rows.append(row.astype(I32))
    return cols, rows


def swap_halves(x, flag):
    n = x.shape[1] // 2
    return jnp.where(flag, jnp.concatenate([x[:, n:], x[:, :n]], 1), x)


def prepare_body(experts, capacity, top, swap, place, ids_ref, num_ref, hid_ref, row_ref, col_ref, send_ref):
    tokens = ids_ref.shape[0]
    units = hid_ref.shape[1] // top
    cols, rows = slot_rows(ids_ref[...], experts, capacity)
    numerators = num_ref[...].astype(F32)
    total = jnp.sum(numerators, axis=1, keepdims=True)
    target = iota((experts * capacity, tokens), 0)
    acc = None
    for k in range(top):
        row_ref[k : k + 1, :] = rows[k]
        col_ref[:, k : k + 1] = cols[k]
        share = numerators[:, k : k + 1] / total
        scaled = (share * hid_ref[:, k * units : (k + 1) * units].astype(F32)).astype(BF16)
        part = dot((target == rows[k]).astype(BF16), scaled)
        acc = part if acc is None else acc + part
    out = acc.astype(BF16)
    send_ref[...] = swap_halves(out, place[1] == 1) if swap else out


def rows_body(experts, capacity, place, *refs):
    ids_refs, row_refs = refs[:PLANES], refs[PLANES:]
    found = [slot_rows(ref[...], experts, capacity)[1] for ref in ids_refs]
    for i, row_ref in enumerate(row_refs):
        for k in range(row_ref.shape[0]):
            row = found[PLANES - 1][k]
            for j in range(PLANES - 1):
                row = jnp.where((place[0] ^ i) == j, found[j][k], row)
            row_ref[k : k + 1, :] = row


def picks(place, peers, capacity, row_refs):
    r = iota((peers * PAIR * capacity, 1), 0)
    peer = r // (PAIR * capacity)
    which = (r // capacity) % PAIR
    target = (place[0] * peers + peer) * capacity + r % capacity
    blocks = []
    for j, row_ref in enumerate(row_refs):
        hit = None
        for k in range(row_ref.shape[0]):
            h = target == row_ref[k : k + 1, :]
            hit = h if hit is None else hit | h
        blocks.append((hit & (which == j)).astype(BF16))
    return jnp.concatenate(blocks, 1)


def pick_body(peers, capacity, offset, place, *refs):
    *row_refs, grad_ref, out_ref = refs
    tokens = row_refs[0].shape[1]
    n = PAIR * capacity
    groups = PLANES // PAIR
    for g in range(groups):
        pick = picks(place, peers, capacity, row_refs[g * PAIR : (g + 1) * PAIR])
        for at in steps(out_ref.shape[1]):
            cols = slice(offset + at.start, offset + at.stop)
            res = dot(pick, grad_ref[g * PAIR * tokens : (g + 1) * PAIR * tokens, cols]).astype(BF16)
            for k in range(peers):
                o = (k * groups + g) * n
                out_ref[o : o + n, at] = res[k * n : (k + 1) * n]


def combine_body(peers, capacity, place, *refs):
    *row_refs, back_ref, out_ref = refs
    tokens = row_refs[0].shape[1]
    n = PAIR * capacity
    groups = PLANES // PAIR
    for g in range(groups):
        pick = picks(place, peers, capacity, row_refs[g * PAIR : (g + 1) * PAIR])
        for at in steps(out_ref.shape[1]):
            rows = [back_ref[(k * groups + g) * n : (k * groups + g + 1) * n, at] for k in range(peers)]
            both = dot(pick, jnp.concatenate(rows, 0), 0, 0).astype(BF16)
            out_ref[g * PAIR * tokens : (g + 1) * PAIR * tokens, at] = both


def reorder(x, outer, inner, capacity):
    return jnp.concatenate(
        [
            x[(a * inner + b) * capacity : (a * inner + b + 1) * capacity]
            for b in range(inner)
            for a in range(outer)
        ],
        0,
    )


def arrange_body(peers, capacity, place, hid_ref, out_ref):
    out_ref[...] = reorder(hid_ref[...].astype(F32), PLANES, peers, capacity).astype(BF16)


def forward_body(offset, place, hid_ref, *refs):
    *weights, out_ref = refs
    hid = hid_ref[...]
    for at in steps(out_ref.shape[1]):
        acc, r = None, 0
        for i, w in enumerate(weights):
            o = offset if i == 0 else 0
            part = dot(hid[:, r : r + w.shape[0]], w[:, o + at.start : o + at.stop])
            acc = part if acc is None else acc + part
            r += w.shape[0]
        out_ref[:, at] = acc.astype(BF16)


def weight_grad_body(lo, hi, place, hid_ref, grad_ref, out_ref):
    for at in steps(out_ref.shape[1]):
        out_ref[:, at] = dot(hid_ref[:, lo:hi], grad_ref[:, at], 0, 0).astype(BF16)


def average_body(replicas, place, *refs):
    *pieces, out_ref = refs
    n = len(pieces) // 2
    c = 0
    for a, b in zip(pieces[:n], pieces[n:]):
        for at in steps(a.shape[1]):
            total = a[:, at].astype(F32) + b[:, at].astype(F32)
            out_ref[:, c + at.start : c + at.stop] = (total / replicas).astype(BF16)
        c += a.shape[1]


def back_dots(grad_ref, weights, offset):
    w = weights[0][:, offset : offset + grad_ref.shape[1]]
    return [dot(grad_ref[...], w, 1, 1)] + [dot(grad_ref[...], x[...], 1, 1) for x in weights[1:]]


def backward_first_body(offset, place, grad_ref, *refs):
    *weights, out_ref = refs
    r = 0
    for part in back_dots(grad_ref, weights, offset):
        out_ref[:, r : r + part.shape[1]] = part
        r += part.shape[1]


def backward_last_body(peers, capacity, offset, place, first_ref, grad_ref, *refs):
    *weights, out_ref = refs
    r = 0
    for part in back_dots(grad_ref, weights, offset):
        m = part.shape[1]
        total = first_ref[:, r : r + m] + part
        out_ref[:, r : r + m] = reorder(total, peers, PLANES, capacity).astype(BF16)
        r += m


def hidden_grad_body(top, swap, place, col_ref, num_ref, back_ref, out_ref):
    tokens = col_ref.shape[0]
    rows, units = back_ref.shape
    numerators = num_ref[...].astype(F32)
    total = jnp.sum(numerators, axis=1, keepdims=True)
    target = iota((tokens, rows), 1)
    for k in range(top):
        hit = (target == col_ref[:, k : k + 1]).astype(BF16)
        got = (numerators[:, k : k + 1] / total * dot(hit, back_ref[...])).astype(BF16)
        out_ref[:, k * units : (k + 1) * units] = swap_halves(got, place[1] == 1) if swap else got


def after(x, *others):
    return lax.optimization_barrier((x, *others))[0]


def exchange(x, axes):
    return lax.all_to_all(x, axes, split_axis=0, concat_axis=0, tiled=True)


def cut(x, n):
    m = x.shape[1] // n
    return [x[:, i * m : (i + 1) * m] for i in range(n)]


def on_device(hidden_in, out_grad, expert_ids, gate_num, down_weight):
    tokens, top, units = hidden_in.shape
    width = out_grad.shape[1]
    peers = lax.axis_size("p")
    experts = PLANES * peers
    replicas = lax.axis_size("dp")
    capacity = 4 * tokens // experts
    share = units // replicas
    pair = replicas == 2
    z = lax.axis_index("z")
    place = jnp.stack([lax.axis_index("z"), lax.axis_index("dp"), lax.axis_index("p")]).astype(I32)
    part = functools.partial
    row_shape, col_shape = shaped((top, tokens), I32), shaped((tokens, top), I32)
    piece = width // 2
    total_rows = experts * capacity

    def to_replica(x):
        return lax.ppermute(x, "dp", [(0, 1), (1, 0)])

    weight = down_weight[0]
    if pair:
        w_a = cut(weight, 2)[0]
        mine = weight
    else:
        theirs = []
        mine = lax.all_gather(weight, "dp", axis=0, tiled=True)

    row_own, col_own, send_hidden = call(
        part(prepare_body, experts, capacity, top, pair),
        [row_shape, col_shape, shaped((total_rows, units))],
        place, expert_ids, gate_num, hidden_in.reshape(tokens, top * units),
    )
    grads = lax.all_gather(out_grad, "z", axis=0, tiled=True)
    if pair:
        theirs = [to_replica(w_a), to_replica(cut(after(weight, send_hidden), 2)[1])]
    hid = exchange(send_hidden, ("z", "p"))
    hid = call(part(arrange_body, peers, capacity), shaped((total_rows, units)), place, hid)
    near = [expert_ids] + [
        lax.ppermute(expert_ids, "z", [(i, i ^ j) for i in range(PLANES)]) for j in range(1, PLANES)
    ]
    chunk = shaped((total_rows, piece))

    def forward(c):
        weights = [mine] + ([theirs[c]] if pair else [])
        return call(part(forward_body, c * piece), chunk, place, hid, *weights, cost=COST)

    def combine(rows, x):
        return call(
            part(combine_body, peers, capacity), shaped((PLANES * tokens, piece)), place, *rows, x
        )

    def reduce(x):
        return lax.psum_scatter(x, "z", scatter_dimension=0, tiled=True)

    def pick(rows, c):
        return call(part(pick_body, peers, capacity, c * piece), chunk, place, *rows, grads, cost=COST)

    def weight_grad(x, lo, hi, cost=0, wait=()):
        return call(
            part(weight_grad_body, lo, hi), shaped((hi - lo, piece)),
            after(place, *wait), hid, x, cost=cost,
        )

    out_a, out_b = forward(0), forward(1)
    done_a = after(exchange(out_a, "p"), out_b)
    done_b = exchange(after(out_b, done_a), "p")
    rows = call(
        part(rows_body, experts, capacity), [row_shape] * PLANES, after(place, done_a), *near
    )
    part_a = combine(rows, done_a)
    pick_a = pick(rows, 0)
    done_b = after(done_b, part_a)
    layer_a = reduce(after(part_a, done_b))
    sent_a = exchange(after(pick_a, done_b), "p")
    part_b = combine(rows, done_b)
    layer_b = reduce(part_b)
    pick_b = pick(rows, 1)
    sent_a = after(sent_a, part_b, pick_b)
    sent_b = exchange(after(pick_b, sent_a), "p")
    lo, hi = (share, units) if pair else (0, units)
    other_a = weight_grad(sent_a, lo, hi)
    own_a = weight_grad(sent_a, 0, share, wait=(other_a,)) if pair else jnp.zeros((share, piece), BF16)
    first = call(
        part(backward_first_body, 0), shaped((total_rows, units), F32), place, sent_a, mine, *theirs[:1]
    )
    sent_b = after(sent_b, other_a, own_a, first)
    other_b = weight_grad(sent_b, lo, hi)
    grad_rows = call(
        part(backward_last_body, peers, capacity, piece), shaped((total_rows, units)),
        after(place, other_b), first, sent_b, mine, *theirs[1:],
    )
    back_rows = exchange(grad_rows, ("z", "p"))
    if pair:
        own_b = weight_grad(after(sent_b, grad_rows), 0, share, cost=COST)
    else:
        own_b = jnp.zeros((share, piece), BF16)
    other_grads, own_grads, back = [other_a, other_b], [own_a, own_b], [layer_a, layer_b]
    if pair:
        other_grads = [to_replica(g) for g in other_grads]
    else:
        other_grads = [
            lax.psum_scatter(g, "dp", scatter_dimension=0, tiled=True) for g in other_grads
        ]

    down_grad = call(
        part(average_body, replicas), shaped((share, width)), after(place, own_b, layer_a), *own_grads, *other_grads
    )
    hidden_grad = call(
        part(hidden_grad_body, top, pair), shaped((tokens, top * units)), after(place, down_grad), col_own, gate_num, back_rows
    )
    layer_out = jnp.concatenate([layer_a, after(layer_b, down_grad)], 1)
    return (layer_out, hidden_grad.reshape(tokens, top, units), down_grad[None])


def solution(mesh):
    replicas, experts = mesh.devices.shape
    planes = Mesh(mesh.devices.reshape(replicas, PLANES, experts // PLANES), ("dp", "z", "p"))
    tokens = ("dp", "z", "p")
    return jax.shard_map(
        on_device,
        mesh=planes,
        in_specs=(
            P(tokens, None, None),
            P(tokens, None),
            P(tokens, None),
            P(tokens, None),
            P(("z", "p"), "dp", None),
        ),
        out_specs=(
            P(tokens, None),
            P(tokens, None, None),
            P(("z", "p"), "dp", None),
        ),
        check_vma=False,
    )
```

```python
import functools

import jax
import jax.numpy as jnp
from jax import lax
from jax.experimental import pallas as pl
from jax.experimental.pallas import tpu as pltpu
from jax.sharding import Mesh
from jax.sharding import PartitionSpec as P

F32 = jnp.float32
BF16 = jnp.bfloat16
I32 = jnp.int32
VMEM = pl.BlockSpec(memory_space=pltpu.VMEM)
SMEM = pl.BlockSpec(memory_space=pltpu.SMEM)
STEP = 1024
PLANES = 4
PAIR = 2
COST = 1 << 38


def dot(a, b, ca=1, cb=0):
    return lax.dot_general(a, b, (((ca,), (cb,)), ((), ())), preferred_element_type=F32)


def call(body, outs, *args, cost=0, scratch=()):
    many = isinstance(outs, (list, tuple))
    return pl.pallas_call(
        body,
        out_shape=outs,
        in_specs=[SMEM] + [VMEM] * (len(args) - 1),
        out_specs=[VMEM] * len(outs) if many else VMEM,
        scratch_shapes=scratch,
        name=(body.func if isinstance(body, functools.partial) else body).__name__,
        cost_estimate=pl.CostEstimate(flops=cost, bytes_accessed=0, transcendentals=0),
        compiler_params=pltpu.CompilerParams(vmem_limit_bytes=16 * 1024 * 1024),
    )(*args)


def shaped(shape, dtype=BF16):
    return jax.ShapeDtypeStruct(tuple(shape), dtype)


def iota(shape, dim):
    return lax.broadcasted_iota(I32, shape, dim)


def steps(width):
    step = min(STEP, width)
    return [slice(c, c + step) for c in range(0, width, step)]


def slot_rows(ids, experts, capacity):
    tokens = ids.shape[0]
    lanes = iota((tokens, experts), 1)
    earlier = (iota((tokens, tokens), 0) > iota((tokens, tokens), 1)).astype(BF16)
    eye = iota((tokens, tokens), 0) == iota((tokens, tokens), 1)
    cols, rows = [], []
    base = jnp.zeros((1, experts), F32)
    for k in range(ids.shape[1]):
        chosen = ids[:, k : k + 1]
        one_hot = (chosen == lanes).astype(F32)
        before = dot(earlier, one_hot.astype(BF16)) + base
        ordinal = jnp.sum(before * one_hot, axis=1, keepdims=True)
        base = base + jnp.sum(one_hot, axis=0, keepdims=True)
        col = chosen.astype(F32) * capacity + ordinal
        row = jnp.sum(jnp.where(eye, jnp.broadcast_to(col, (tokens, tokens)), 0.0), axis=0, keepdims=True)
        cols.append(col.astype(I32))
        rows.append(row.astype(I32))
    return cols, rows


def swap_halves(x, flag):
    n = x.shape[1] // 2
    return jnp.where(flag, jnp.concatenate([x[:, n:], x[:, :n]], 1), x)


def prepare_body(experts, capacity, top, swap, place, ids_ref, num_ref, hid_ref, row_ref, col_ref, send_ref):
    tokens = ids_ref.shape[0]
    units = hid_ref.shape[1] // top
    cols, rows = slot_rows(ids_ref[...], experts, capacity)
    numerators = num_ref[...].astype(F32)
    total = jnp.sum(numerators, axis=1, keepdims=True)
    target = iota((experts * capacity, tokens), 0)
    acc = None
    for k in range(top):
        row_ref[k : k + 1, :] = rows[k]
        col_ref[:, k : k + 1] = cols[k]
        share = numerators[:, k : k + 1] / total
        scaled = (share * hid_ref[:, k * units : (k + 1) * units].astype(F32)).astype(BF16)
        part = dot((target == rows[k]).astype(BF16), scaled)
        acc = part if acc is None else acc + part
    out = acc.astype(BF16)
    send_ref[...] = swap_halves(out, place[1] == 1) if swap else out


def rows_body(experts, capacity, place, *refs):
    ids_refs, row_refs = refs[:PLANES], refs[PLANES:]
    found = [slot_rows(ref[...], experts, capacity)[1] for ref in ids_refs]
    for i, row_ref in enumerate(row_refs):
        for k in range(row_ref.shape[0]):
            row = found[PLANES - 1][k]
            for j in range(PLANES - 1):
                row = jnp.where((place[0] ^ i) == j, found[j][k], row)
            row_ref[k : k + 1, :] = row


def picks(place, peers, capacity, row_refs):
    r = iota((peers * PAIR * capacity, 1), 0)
    peer = r // (PAIR * capacity)
    which = (r // capacity) % PAIR
    target = (place[0] * peers + peer) * capacity + r % capacity
    blocks = []
    for j, row_ref in enumerate(row_refs):
        hit = None
        for k in range(row_ref.shape[0]):
            h = target == row_ref[k : k + 1, :]
            hit = h if hit is None else hit | h
        blocks.append((hit & (which == j)).astype(BF16))
    return jnp.concatenate(blocks, 1)


def pick_body(peers, capacity, offset, place, *refs):
    *row_refs, grad_ref, out_ref = refs
    tokens = row_refs[0].shape[1]
    n = PAIR * capacity
    groups = PLANES // PAIR
    for g in range(groups):
        pick = picks(place, peers, capacity, row_refs[g * PAIR : (g + 1) * PAIR])
        for at in steps(out_ref.shape[1]):
            cols = slice(offset + at.start, offset + at.stop)
            res = dot(pick, grad_ref[g * PAIR * tokens : (g + 1) * PAIR * tokens, cols]).astype(BF16)
            for k in range(peers):
                o = (k * groups + g) * n
                out_ref[o : o + n, at] = res[k * n : (k + 1) * n]


def combine_body(peers, capacity, place, *refs):
    *row_refs, back_ref, out_ref = refs
    tokens = row_refs[0].shape[1]
    n = PAIR * capacity
    groups = PLANES // PAIR
    for g in range(groups):
        pick = picks(place, peers, capacity, row_refs[g * PAIR : (g + 1) * PAIR])
        for at in steps(out_ref.shape[1]):
            rows = [back_ref[(k * groups + g) * n : (k * groups + g + 1) * n, at] for k in range(peers)]
            both = dot(pick, jnp.concatenate(rows, 0), 0, 0).astype(BF16)
            out_ref[g * PAIR * tokens : (g + 1) * PAIR * tokens, at] = both


def reorder(x, outer, inner, capacity):
    return jnp.concatenate(
        [
            x[(a * inner + b) * capacity : (a * inner + b + 1) * capacity]
            for b in range(inner)
            for a in range(outer)
        ],
        0,
    )


def arrange_body(peers, capacity, place, hid_ref, out_ref):
    out_ref[...] = reorder(hid_ref[...].astype(F32), PLANES, peers, capacity).astype(BF16)


def forward_body(offset, place, hid_ref, *refs):
    *weights, out_ref = refs
    hid = hid_ref[...]
    for at in steps(out_ref.shape[1]):
        acc, r = None, 0
        for i, w in enumerate(weights):
            o = offset if i == 0 else 0
            part = dot(hid[:, r : r + w.shape[0]], w[:, o + at.start : o + at.stop])
            acc = part if acc is None else acc + part
            r += w.shape[0]
        out_ref[:, at] = acc.astype(BF16)


def weight_grad_body(lo, hi, place, hid_ref, grad_ref, out_ref):
    for at in steps(out_ref.shape[1]):
        out_ref[:, at] = dot(hid_ref[:, lo:hi], grad_ref[:, at], 0, 0).astype(BF16)


def back_dots(grad_ref, weights, offset):
    w = weights[0][:, offset : offset + grad_ref.shape[1]]
    return [dot(grad_ref[...], w, 1, 1)] + [dot(grad_ref[...], x[...], 1, 1) for x in weights[1:]]


def backward_first_body(offset, place, grad_ref, *refs):
    *weights, out_ref = refs
    r = 0
    for part in back_dots(grad_ref, weights, offset):
        out_ref[:, r : r + part.shape[1]] = part
        r += part.shape[1]


def backward_last_body(peers, capacity, offset, place, first_ref, grad_ref, *refs):
    *weights, out_ref = refs
    r = 0
    for part in back_dots(grad_ref, weights, offset):
        m = part.shape[1]
        total = first_ref[:, r : r + m] + part
        out_ref[:, r : r + m] = reorder(total, peers, PLANES, capacity).astype(BF16)
        r += m


def hidden_grad_body(top, swap, place, col_ref, num_ref, back_ref, out_ref):
    tokens = col_ref.shape[0]
    rows, units = back_ref.shape
    numerators = num_ref[...].astype(F32)
    total = jnp.sum(numerators, axis=1, keepdims=True)
    target = iota((tokens, rows), 1)
    for k in range(top):
        hit = (target == col_ref[:, k : k + 1]).astype(BF16)
        got = (numerators[:, k : k + 1] / total * dot(hit, back_ref[...])).astype(BF16)
        out_ref[:, k * units : (k + 1) * units] = swap_halves(got, place[1] == 1) if swap else got


def after(x, *others):
    return lax.optimization_barrier((x, *others))[0]


def exchange(x, axes):
    return lax.all_to_all(x, axes, split_axis=0, concat_axis=0, tiled=True)


def cut(x, n):
    m = x.shape[1] // n
    return [x[:, i * m : (i + 1) * m] for i in range(n)]


def on_device(hidden_in, out_grad, expert_ids, gate_num, down_weight):
    tokens, top, units = hidden_in.shape
    width = out_grad.shape[1]
    peers = lax.axis_size("p")
    experts = PLANES * peers
    replicas = lax.axis_size("dp")
    capacity = 4 * tokens // experts
    share = units // replicas
    pair = replicas == 2
    z = lax.axis_index("z")
    place = jnp.stack([lax.axis_index("z"), lax.axis_index("dp"), lax.axis_index("p")]).astype(I32)
    part = functools.partial
    row_shape, col_shape = shaped((top, tokens), I32), shaped((tokens, top), I32)
    piece = width // 2
    total_rows = experts * capacity

    def to_replica(x):
        return lax.ppermute(x, "dp", [(0, 1), (1, 0)])

    weight = down_weight[0]
    if pair:
        w_a = cut(weight, 2)[0]
        mine = weight
    else:
        theirs = []
        mine = lax.all_gather(weight, "dp", axis=0, tiled=True)

    row_own, col_own, send_hidden = call(
        part(prepare_body, experts, capacity, top, pair),
        [row_shape, col_shape, shaped((total_rows, units))],
        place, expert_ids, gate_num, hidden_in.reshape(tokens, top * units),
    )
    grads = lax.all_gather(out_grad, "z", axis=0, tiled=True)
    if pair:
        theirs = [to_replica(w_a), to_replica(cut(after(weight, send_hidden), 2)[1])]
    hid = exchange(send_hidden, ("z", "p"))
    hid = call(part(arrange_body, peers, capacity), shaped((total_rows, units)), place, hid)
    near = [expert_ids] + [
        lax.ppermute(expert_ids, "z", [(i, i ^ j) for i in range(PLANES)]) for j in range(1, PLANES)
    ]
    chunk = shaped((total_rows, piece))

    def forward(c):
        weights = [mine] + ([theirs[c]] if pair else [])
        return call(part(forward_body, c * piece), chunk, place, hid, *weights, cost=COST)

    def combine(rows, x):
        return call(
            part(combine_body, peers, capacity), shaped((PLANES * tokens, piece)), place, *rows, x
        )

    def reduce(x):
        return lax.psum_scatter(x, "z", scatter_dimension=0, tiled=True)

    def pick(rows, c):
        return call(part(pick_body, peers, capacity, c * piece), chunk, place, *rows, grads, cost=COST)

    def weight_grad(x, lo, hi, cost=0, wait=()):
        return call(
            part(weight_grad_body, lo, hi), shaped((hi - lo, piece)),
            after(place, *wait), hid, x, cost=cost,
        )

    out_a, out_b = forward(0), forward(1)
    done_a = after(exchange(out_a, "p"), out_b)
    done_b = exchange(after(out_b, done_a), "p")
    rows = call(
        part(rows_body, experts, capacity), [row_shape] * PLANES, after(place, done_a), *near
    )
    part_a = combine(rows, done_a)
    pick_a = pick(rows, 0)
    done_b = after(done_b, part_a)
    layer_a = reduce(after(part_a, done_b))
    sent_a = exchange(after(pick_a, done_b), "p")
    part_b = combine(rows, done_b)
    layer_b = reduce(part_b)
    pick_b = pick(rows, 1)
    sent_a = after(sent_a, part_b, pick_b)
    sent_b = exchange(after(pick_b, sent_a), "p")
    lo, hi = (share, units) if pair else (0, units)
    other_a = weight_grad(sent_a, lo, hi)
    own_a = weight_grad(sent_a, 0, share, wait=(other_a,)) if pair else jnp.zeros((share, piece), BF16)
    first = call(
        part(backward_first_body, 0), shaped((total_rows, units), F32), place, sent_a, mine, *theirs[:1]
    )
    sent_b = after(sent_b, other_a, own_a, first)
    other_b = weight_grad(sent_b, lo, hi)
    grad_rows = call(
        part(backward_last_body, peers, capacity, piece), shaped((total_rows, units)),
        after(place, other_b), first, sent_b, mine, *theirs[1:],
    )
    back_rows = exchange(grad_rows, ("z", "p"))
    if pair:
        own_b = weight_grad(after(sent_b, grad_rows), 0, share, cost=COST)
    else:
        own_b = jnp.zeros((share, piece), BF16)
    other_grads, own_grads, back = [other_a, other_b], [own_a, own_b], [layer_a, layer_b]
    if pair:
        other_grads = [to_replica(g) for g in other_grads]
    else:
        other_grads = [
            lax.psum_scatter(g, "dp", scatter_dimension=0, tiled=True) for g in other_grads
        ]

    down_grad = jnp.concatenate(
        [
            ((own.astype(F32) + after(other, own_b, layer_a).astype(F32)) / replicas).astype(BF16)
            for own, other in zip(own_grads, other_grads)
        ],
        1,
    )
    hidden_grad = call(
        part(hidden_grad_body, top, pair), shaped((tokens, top * units)), after(place, down_grad), col_own, gate_num, back_rows
    )
    layer_out = jnp.concatenate([layer_a, after(layer_b, down_grad)], 1)
    return (layer_out, hidden_grad.reshape(tokens, top, units), down_grad[None])


def solution(mesh):
    replicas, experts = mesh.devices.shape
    planes = Mesh(mesh.devices.reshape(replicas, PLANES, experts // PLANES), ("dp", "z", "p"))
    tokens = ("dp", "z", "p")
    return jax.shard_map(
        on_device,
        mesh=planes,
        in_specs=(
            P(tokens, None, None),
            P(tokens, None),
            P(tokens, None),
            P(tokens, None),
            P(("z", "p"), "dp", None),
        ),
        out_specs=(
            P(tokens, None),
            P(tokens, None, None),
            P(("z", "p"), "dp", None),
        ),
        check_vma=False,
    )
```

```python
import functools

import jax
import jax.numpy as jnp
from jax import lax
from jax.experimental import pallas as pl
from jax.experimental.pallas import tpu as pltpu
from jax.sharding import Mesh
from jax.sharding import PartitionSpec as P

F32 = jnp.float32
BF16 = jnp.bfloat16
I32 = jnp.int32
VMEM = pl.BlockSpec(memory_space=pltpu.VMEM)
SMEM = pl.BlockSpec(memory_space=pltpu.SMEM)
STEP = 1024
PLANES = 4
PAIR = 2
COST = 1 << 38


def dot(a, b, ca=1, cb=0):
    return lax.dot_general(a, b, (((ca,), (cb,)), ((), ())), preferred_element_type=F32)


def call(body, outs, *args, cost=0, scratch=()):
    many = isinstance(outs, (list, tuple))
    return pl.pallas_call(
        body,
        out_shape=outs,
        in_specs=[SMEM] + [VMEM] * (len(args) - 1),
        out_specs=[VMEM] * len(outs) if many else VMEM,
        scratch_shapes=scratch,
        name=(body.func if isinstance(body, functools.partial) else body).__name__,
        cost_estimate=pl.CostEstimate(flops=cost, bytes_accessed=0, transcendentals=0),
        compiler_params=pltpu.CompilerParams(vmem_limit_bytes=8 * 1024 * 1024),
    )(*args)


def shaped(shape, dtype=BF16):
    return jax.ShapeDtypeStruct(tuple(shape), dtype)


def iota(shape, dim):
    return lax.broadcasted_iota(I32, shape, dim)


def steps(width):
    step = min(STEP, width)
    return [slice(c, c + step) for c in range(0, width, step)]


def slot_rows(ids, experts, capacity):
    tokens = ids.shape[0]
    lanes = iota((tokens, experts), 1)
    earlier = (iota((tokens, tokens), 0) > iota((tokens, tokens), 1)).astype(BF16)
    eye = iota((tokens, tokens), 0) == iota((tokens, tokens), 1)
    cols, rows = [], []
    base = jnp.zeros((1, experts), F32)
    for k in range(ids.shape[1]):
        chosen = ids[:, k : k + 1]
        one_hot = (chosen == lanes).astype(F32)
        before = dot(earlier, one_hot.astype(BF16)) + base
        ordinal = jnp.sum(before * one_hot, axis=1, keepdims=True)
        base = base + jnp.sum(one_hot, axis=0, keepdims=True)
        col = chosen.astype(F32) * capacity + ordinal
        row = jnp.sum(jnp.where(eye, jnp.broadcast_to(col, (tokens, tokens)), 0.0), axis=0, keepdims=True)
        cols.append(col.astype(I32))
        rows.append(row.astype(I32))
    return cols, rows


def swap_halves(x, flag):
    n = x.shape[1] // 2
    return jnp.where(flag, jnp.concatenate([x[:, n:], x[:, :n]], 1), x)


def prepare_body(experts, capacity, top, swap, place, ids_ref, num_ref, hid_ref, row_ref, col_ref, send_ref):
    tokens = ids_ref.shape[0]
    units = hid_ref.shape[1] // top
    cols, rows = slot_rows(ids_ref[...], experts, capacity)
    numerators = num_ref[...].astype(F32)
    total = jnp.sum(numerators, axis=1, keepdims=True)
    target = iota((experts * capacity, tokens), 0)
    acc = None
    for k in range(top):
        row_ref[k : k + 1, :] = rows[k]
        col_ref[:, k : k + 1] = cols[k]
        share = numerators[:, k : k + 1] / total
        scaled = (share * hid_ref[:, k * units : (k + 1) * units].astype(F32)).astype(BF16)
        part = dot((target == rows[k]).astype(BF16), scaled)
        acc = part if acc is None else acc + part
    out = acc.astype(BF16)
    send_ref[...] = swap_halves(out, place[1] == 1) if swap else out


def rows_body(experts, capacity, place, *refs):
    ids_refs, row_refs = refs[:PLANES], refs[PLANES:]
    found = [slot_rows(ref[...], experts, capacity)[1] for ref in ids_refs]
    for i, row_ref in enumerate(row_refs):
        for k in range(row_ref.shape[0]):
            row = found[PLANES - 1][k]
            for j in range(PLANES - 1):
                row = jnp.where((place[0] ^ i) == j, found[j][k], row)
            row_ref[k : k + 1, :] = row


def picks(place, peers, capacity, row_refs):
    r = iota((peers * PAIR * capacity, 1), 0)
    peer = r // (PAIR * capacity)
    which = (r // capacity) % PAIR
    target = (place[0] * peers + peer) * capacity + r % capacity
    blocks = []
    for j, row_ref in enumerate(row_refs):
        hit = None
        for k in range(row_ref.shape[0]):
            h = target == row_ref[k : k + 1, :]
            hit = h if hit is None else hit | h
        blocks.append((hit & (which == j)).astype(BF16))
    return jnp.concatenate(blocks, 1)


def pick_body(peers, capacity, offset, place, *refs):
    *row_refs, grad_ref, out_ref = refs
    tokens = row_refs[0].shape[1]
    n = PAIR * capacity
    groups = PLANES // PAIR
    for g in range(groups):
        pick = picks(place, peers, capacity, row_refs[g * PAIR : (g + 1) * PAIR])
        for at in steps(out_ref.shape[1]):
            cols = slice(offset + at.start, offset + at.stop)
            res = dot(pick, grad_ref[g * PAIR * tokens : (g + 1) * PAIR * tokens, cols]).astype(BF16)
            for k in range(peers):
                o = (k * groups + g) * n
                out_ref[o : o + n, at] = res[k * n : (k + 1) * n]


def combine_body(peers, capacity, place, *refs):
    *row_refs, back_ref, out_ref = refs
    tokens = row_refs[0].shape[1]
    n = PAIR * capacity
    groups = PLANES // PAIR
    for g in range(groups):
        pick = picks(place, peers, capacity, row_refs[g * PAIR : (g + 1) * PAIR])
        for at in steps(out_ref.shape[1]):
            rows = [back_ref[(k * groups + g) * n : (k * groups + g + 1) * n, at] for k in range(peers)]
            both = dot(pick, jnp.concatenate(rows, 0), 0, 0).astype(BF16)
            out_ref[g * PAIR * tokens : (g + 1) * PAIR * tokens, at] = both


def reorder(x, outer, inner, capacity):
    return jnp.concatenate(
        [
            x[(a * inner + b) * capacity : (a * inner + b + 1) * capacity]
            for b in range(inner)
            for a in range(outer)
        ],
        0,
    )


def arrange_body(peers, capacity, place, hid_ref, out_ref):
    out_ref[...] = reorder(hid_ref[...].astype(F32), PLANES, peers, capacity).astype(BF16)


def forward_body(offset, place, hid_ref, *refs):
    *weights, out_ref = refs
    hid = hid_ref[...]
    for at in steps(out_ref.shape[1]):
        acc, r = None, 0
        for i, w in enumerate(weights):
            o = offset if i == 0 else 0
            part = dot(hid[:, r : r + w.shape[0]], w[:, o + at.start : o + at.stop])
            acc = part if acc is None else acc + part
            r += w.shape[0]
        out_ref[:, at] = acc.astype(BF16)


def weight_grad_body(lo, hi, place, hid_ref, grad_ref, out_ref):
    for at in steps(out_ref.shape[1]):
        out_ref[:, at] = dot(hid_ref[:, lo:hi], grad_ref[:, at], 0, 0).astype(BF16)


def back_dots(grad_ref, weights, offset):
    w = weights[0][:, offset : offset + grad_ref.shape[1]]
    return [dot(grad_ref[...], w, 1, 1)] + [dot(grad_ref[...], x[...], 1, 1) for x in weights[1:]]


def backward_first_body(offset, place, grad_ref, *refs):
    *weights, out_ref = refs
    r = 0
    for part in back_dots(grad_ref, weights, offset):
        out_ref[:, r : r + part.shape[1]] = part
        r += part.shape[1]


def backward_last_body(peers, capacity, offset, place, first_ref, grad_ref, *refs):
    *weights, out_ref = refs
    r = 0
    for part in back_dots(grad_ref, weights, offset):
        m = part.shape[1]
        total = first_ref[:, r : r + m] + part
        out_ref[:, r : r + m] = reorder(total, peers, PLANES, capacity).astype(BF16)
        r += m


def hidden_grad_body(top, swap, place, col_ref, num_ref, back_ref, out_ref):
    tokens = col_ref.shape[0]
    rows, units = back_ref.shape
    numerators = num_ref[...].astype(F32)
    total = jnp.sum(numerators, axis=1, keepdims=True)
    target = iota((tokens, rows), 1)
    for k in range(top):
        hit = (target == col_ref[:, k : k + 1]).astype(BF16)
        got = (numerators[:, k : k + 1] / total * dot(hit, back_ref[...])).astype(BF16)
        out_ref[:, k * units : (k + 1) * units] = swap_halves(got, place[1] == 1) if swap else got


def after(x, *others):
    return lax.optimization_barrier((x, *others))[0]


def exchange(x, axes):
    return lax.all_to_all(x, axes, split_axis=0, concat_axis=0, tiled=True)


def cut(x, n):
    m = x.shape[1] // n
    return [x[:, i * m : (i + 1) * m] for i in range(n)]


def on_device(hidden_in, out_grad, expert_ids, gate_num, down_weight):
    tokens, top, units = hidden_in.shape
    width = out_grad.shape[1]
    peers = lax.axis_size("p")
    experts = PLANES * peers
    replicas = lax.axis_size("dp")
    capacity = 4 * tokens // experts
    share = units // replicas
    pair = replicas == 2
    z = lax.axis_index("z")
    place = jnp.stack([lax.axis_index("z"), lax.axis_index("dp"), lax.axis_index("p")]).astype(I32)
    part = functools.partial
    row_shape, col_shape = shaped((top, tokens), I32), shaped((tokens, top), I32)
    piece = width // 2
    total_rows = experts * capacity

    def to_replica(x):
        return lax.ppermute(x, "dp", [(0, 1), (1, 0)])

    weight = down_weight[0]
    if pair:
        w_a = cut(weight, 2)[0]
        mine = weight
    else:
        theirs = []
        mine = lax.all_gather(weight, "dp", axis=0, tiled=True)

    row_own, col_own, send_hidden = call(
        part(prepare_body, experts, capacity, top, pair),
        [row_shape, col_shape, shaped((total_rows, units))],
        place, expert_ids, gate_num, hidden_in.reshape(tokens, top * units),
    )
    grads = lax.all_gather(out_grad, "z", axis=0, tiled=True)
    if pair:
        theirs = [to_replica(w_a), to_replica(cut(after(weight, send_hidden), 2)[1])]
    hid = exchange(send_hidden, ("z", "p"))
    hid = call(part(arrange_body, peers, capacity), shaped((total_rows, units)), place, hid)
    near = [expert_ids] + [
        lax.ppermute(expert_ids, "z", [(i, i ^ j) for i in range(PLANES)]) for j in range(1, PLANES)
    ]
    chunk = shaped((total_rows, piece))

    def forward(c):
        weights = [mine] + ([theirs[c]] if pair else [])
        return call(part(forward_body, c * piece), chunk, place, hid, *weights, cost=COST)

    def combine(rows, x):
        return call(
            part(combine_body, peers, capacity), shaped((PLANES * tokens, piece)), place, *rows, x
        )

    def reduce(x):
        return lax.psum_scatter(x, "z", scatter_dimension=0, tiled=True)

    def pick(rows, c):
        return call(part(pick_body, peers, capacity, c * piece), chunk, place, *rows, grads, cost=COST)

    def weight_grad(x, lo, hi, cost=0, wait=()):
        return call(
            part(weight_grad_body, lo, hi), shaped((hi - lo, piece)),
            after(place, *wait), hid, x, cost=cost,
        )

    out_a, out_b = forward(0), forward(1)
    done_a = after(exchange(out_a, "p"), out_b)
    done_b = exchange(after(out_b, done_a), "p")
    rows = call(
        part(rows_body, experts, capacity), [row_shape] * PLANES, after(place, done_a), *near
    )
    part_a = combine(rows, done_a)
    pick_a = pick(rows, 0)
    done_b = after(done_b, part_a)
    layer_a = reduce(after(part_a, done_b))
    sent_a = exchange(after(pick_a, done_b), "p")
    part_b = combine(rows, done_b)
    layer_b = reduce(part_b)
    pick_b = pick(rows, 1)
    sent_a = after(sent_a, part_b, pick_b)
    sent_b = exchange(after(pick_b, sent_a), "p")
    lo, hi = (share, units) if pair else (0, units)
    other_a = weight_grad(sent_a, lo, hi)
    own_a = weight_grad(sent_a, 0, share, wait=(other_a,)) if pair else jnp.zeros((share, piece), BF16)
    first = call(
        part(backward_first_body, 0), shaped((total_rows, units), F32), place, sent_a, mine, *theirs[:1]
    )
    sent_b = after(sent_b, other_a, own_a, first)
    other_b = weight_grad(sent_b, lo, hi)
    grad_rows = call(
        part(backward_last_body, peers, capacity, piece), shaped((total_rows, units)),
        after(place, other_b), first, sent_b, mine, *theirs[1:],
    )
    back_rows = exchange(grad_rows, ("z", "p"))
    if pair:
        own_b = weight_grad(after(sent_b, grad_rows), 0, share, cost=COST)
    else:
        own_b = jnp.zeros((share, piece), BF16)
    other_grads, own_grads, back = [other_a, other_b], [own_a, own_b], [layer_a, layer_b]
    if pair:
        other_grads = [to_replica(g) for g in other_grads]
    else:
        other_grads = [
            lax.psum_scatter(g, "dp", scatter_dimension=0, tiled=True) for g in other_grads
        ]

    down_grad = jnp.concatenate(
        [
            ((own.astype(F32) + after(other, own_b, layer_a).astype(F32)) / replicas).astype(BF16)
            for own, other in zip(own_grads, other_grads)
        ],
        1,
    )
    hidden_grad = call(
        part(hidden_grad_body, top, pair), shaped((tokens, top * units)), after(place, down_grad), col_own, gate_num, back_rows
    )
    layer_out = jnp.concatenate([layer_a, after(layer_b, down_grad)], 1)
    return (layer_out, hidden_grad.reshape(tokens, top, units), down_grad[None])


def solution(mesh):
    replicas, experts = mesh.devices.shape
    planes = Mesh(mesh.devices.reshape(replicas, PLANES, experts // PLANES), ("dp", "z", "p"))
    tokens = ("dp", "z", "p")
    return jax.shard_map(
        on_device,
        mesh=planes,
        in_specs=(
            P(tokens, None, None),
            P(tokens, None),
            P(tokens, None),
            P(tokens, None),
            P(("z", "p"), "dp", None),
        ),
        out_specs=(
            P(tokens, None),
            P(tokens, None, None),
            P(("z", "p"), "dp", None),
        ),
        check_vma=False,
    )
```
